32 devices in a mesh: dp: 8 (over y, x, core), shard: 4 (over z).
Axes of the slice: x: 2, y: 2, z: 4, core: 2. Of those that a mesh axis runs over, the one named last changes fastest.
Arguments:
- grad_parts: bfloat16 [8, 8, 128, 16384], P('dp', None, 'shard'), may hold values from -6 to 6
- first_moment: float32 [1024, 16384], P(('dp', 'shard')), may hold values from -6 to 6
- second_moment: float32 [1024, 16384], P(('dp', 'shard')), may hold values from 0.1 to 16
- master: float32 [1024, 16384], P(('dp', 'shard')), may hold values from -6 to 6
- old_map: int32 [1024], replicated, may hold values from 0 to 1023, as said below
- new_map: int32 [1024], replicated, may hold values from 0 to 1023, as said below
Outputs:
- new_first: float32 [1024, 16384], P(('dp', 'shard'))
- new_second: float32 [1024, 16384], P(('dp', 'shard'))
- new_master: float32 [1024, 16384], P(('dp', 'shard'))
- weights_half: bfloat16 [1024, 16384], P('dp')
The draws below stay inside these ranges and needn't reach their ends.
Inputs may be any that keep to these rules, and one draw needn't show every extreme that they name: old_map is a permutation of the 1024 block numbers. Row r of either layout belongs to device r // 32. Of the blocks that one device holds in the old layout, exactly one belongs to each device in the new layout. new_map is a permutation of the 1024 block numbers, with the property stated for old_map.
All inputs are finite; a program needn't handle non-finite values.
Results may differ from the reference program's by a relative error of at most 0.0085.
Values may be sent and summed in bfloat16 or wider, within the bound.
No kernel may reach another device: no remote copies, remote signals or barrier semaphores. Data moves between devices by JAX's collectives and lax.ppermute only.
A program may use at most 128 MiB of HBM per device.

```python
import math
import jax
import jax.numpy as jnp
from jax import lax

BPD = 32
BLK = 16384
BLOCKS = 1024
N_DP = 8
N_SHARD = 4


def shuffle_rows(subkey, table):
    side = table.shape[0]
    orders = jax.vmap(lambda inner: jax.random.permutation(inner, table.shape[1]))(jax.random.split(subkey, side))
    return jnp.take_along_axis(table, orders, axis=1)


def relayout_maps(key):
    key_list = jax.random.split(jax.random.fold_in(key, 7), 5)
    side = BPD
    row_perm = jax.random.permutation(key_list[0], side)
    col_perm = jax.random.permutation(key_list[1], side)
    dests = (row_perm[:, None] + col_perm[None, :]) % side
    dests = shuffle_rows(key_list[2], dests)
    flat_dest = dests.reshape(-1)
    labels = jax.random.permutation(key_list[3], BPD * BPD)
    grouped = jnp.argsort(flat_dest, stable=True).reshape(BPD, BPD)
    grouped = shuffle_rows(key_list[4], grouped)
    return (labels.astype(jnp.int32), labels[grouped.reshape(-1)].astype(jnp.int32))


def draw_old_map(key, part):
    return relayout_maps(key)[0]


def draw_new_map(key, part):
    return relayout_maps(key)[1]


def with_spikes(entries, own_key, source, target, shards_of, factor):
    owner, partner = [(jnp.arange(entries.shape[axis_at]) // (entries.shape[axis_at] // shards_of)).reshape([-1 if axis == axis_at else 1 for axis in range(entries.ndim)]) for axis_at in (source, target)]
    chosen = jax.random.permutation(own_key, shards_of)[partner]
    strong = (owner == chosen) | (owner == (partner + shards_of // 2) % shards_of)
    return jnp.where(strong, factor * entries, entries)


def levels(stream_key, extent, shards, least, top_value):
    factor_of, own = 1.0, jax.random.fold_in(stream_key, 6)
    for dim, parts in shards:
        draws = jnp.exp(jax.random.uniform(jax.random.fold_in(own, dim), (parts,), jnp.float32, least / len(shards), top_value / len(shards)))
        factor_of = factor_of * jnp.repeat(draws, extent[dim] // parts).reshape([-1 if axis == dim else 1 for axis in range(len(extent))])
    return factor_of


def centred(key, extent, deviation, most, cuts=(), kind=jnp.bfloat16):
    values = jax.random.normal(key, extent, jnp.float32) * deviation
    if len(cuts) > 0:
        values = levels(key, extent, cuts, -0.22, 0.18) * values
    return jnp.clip(values, min=-most, max=most).astype(kind)


def heavy_noise(own_key, dims, scale, limit, cuts, heavy, kind=jnp.bfloat16):
    result = scale * jax.random.normal(own_key, dims, jnp.float32)
    if cuts:
        result = result * levels(own_key, dims, cuts, -0.22, 0.18)
    return jnp.clip(with_spikes(result, jax.random.fold_in(own_key, 3), *heavy), -limit, limit).astype(kind)


def setup_inputs(seed: int = 0) -> dict:
    splits = jax.random.split(jax.random.key(seed), 7)
    return {
        "grad_parts": heavy_noise(splits[0], (N_DP, N_DP, N_SHARD * BPD, BLK), 1.0, 6.0, ((0, 8), (2, 4)), (0, 1, 8, 2.0)),
        "first_moment": centred(splits[1], (BLOCKS, BLK), 1.0, 6.0, ((0, 32),), jnp.float32),
        "second_moment": jnp.clip(jnp.exp(math.log(16.0) - 5.075174 * jax.random.uniform(splits[2], (BLOCKS, BLK), jnp.float32) ** levels(splits[2], (BLOCKS, BLK), ((0, 32),), -0.2, 0.2)), 0.1, 16.0),
        "master": centred(splits[3], (BLOCKS, BLK), 1.0, 6.0, ((0, 32),), jnp.float32),
        "old_map": draw_old_map(jax.random.fold_in(splits[6], 71), 0),
        "new_map": draw_new_map(jax.random.fold_in(splits[6], 71), 0),
    }


beta_one = 0.9
beta_two = 0.95
learning_rate = 0.05
decay_rate = 0.1
epsilon = 1e-08
step_count = 4

def adamw(moment_one, moment_two, weights, gradient):
    new_one = beta_one * moment_one + (1.0 - beta_one) * gradient
    new_two = beta_two * moment_two + (1.0 - beta_two) * gradient * gradient
    unbiased_one = new_one / (1.0 - beta_one ** step_count)
    unbiased_two = new_two / (1.0 - beta_two ** step_count)
    updated = weights - learning_rate * (unbiased_one / (jnp.sqrt(unbiased_two) + epsilon) + decay_rate * weights)
    return (new_one, new_two, updated)

def reference(grad_parts, first_moment, second_moment, master, old_map, new_map):

    def add_part(index, running):
        piece = lax.dynamic_index_in_dim(grad_parts, index, 0, keepdims=False)
        return running + piece.astype(jnp.float32)
    summed = lax.fori_loop(0, grad_parts.shape[0], add_part, jnp.zeros(grad_parts.shape[1:], jnp.float32))
    summed = summed.reshape(-1, summed.shape[-1])
    row_count = old_map.shape[0]
    old_place = jnp.zeros((row_count,), jnp.int32).at[old_map].set(jnp.arange(row_count, dtype=jnp.int32))
    source = old_place[new_map].astype(jnp.int32)
    new_one, new_two, updated = adamw(first_moment[source], second_moment[source], master[source], summed)
    return (new_one, new_two, updated, updated.astype(jnp.bfloat16))
```

```python
import jax
import jax.numpy as jnp
from jax import lax
from jax.sharding import PartitionSpec as P


beta_one = 0.9
beta_two = 0.95
learning_rate = 0.05
decay_rate = 0.1
epsilon = 1e-08
step_count = 4
LANES = 128
half = jnp.bfloat16
full = jnp.float32


def adamw(moment_one, moment_two, weights, gradient):
    new_one = beta_one * moment_one + (1.0 - beta_one) * gradient
    new_two = beta_two * moment_two + (1.0 - beta_two) * gradient * gradient
    unbiased_one = new_one / (1.0 - beta_one**step_count)
    unbiased_two = new_two / (1.0 - beta_two**step_count)
    updated = weights - learning_rate * (
        unbiased_one / (jnp.sqrt(unbiased_two) + epsilon) + decay_rate * weights
    )
    return (new_one, new_two, updated)


def owner_table(blocks, mapping, device_count, span):
    grid = mapping.reshape(device_count, span)
    found = jnp.any(blocks[:, None, None] == grid[None, :, :], axis=2)
    return found.astype(half)


def sum_over_replicas(grads):
    groups, _, width = grads.shape
    bits = groups.bit_length() - 1
    first = reduce_pair(grads)
    cut = width // 2
    rest = list(range(1, bits))
    return jnp.concatenate(
        [finish(first[..., :cut], rest), finish(first[..., cut:], rest[::-1])], axis=-1
    )


def reduce_pair(grads):
    groups = grads.shape[0]
    mine = lax.axis_index("dp") & 1
    part = grads.reshape((groups // 2, 2) + grads.shape[1:])
    sent = lax.dynamic_index_in_dim(part, 1 - mine, 1, keepdims=False)
    kept = lax.dynamic_index_in_dim(part, mine, 1, keepdims=False)
    came = lax.ppermute(sent, "dp", [(i, i ^ 1) for i in range(groups)])
    return (kept.astype(full) + came.astype(full)).astype(half)


def finish(part, order):
    groups = lax.axis_size("dp")
    mine = lax.axis_index("dp")
    left = sorted(order, reverse=True)
    part = part.reshape((2,) * len(left) + part.shape[1:])
    for bit in order:
        axis = left.index(bit)
        value = (mine >> bit) & 1
        sent = lax.dynamic_index_in_dim(part, 1 - value, axis, keepdims=False).astype(half)
        kept = lax.dynamic_index_in_dim(part, value, axis, keepdims=False)
        came = lax.ppermute(sent, "dp", [(i, i ^ (1 << bit)) for i in range(groups)])
        part = kept.astype(full) + came.astype(full)
        left.remove(bit)
    return part


def gather_line(block):
    n = lax.axis_size("shard")
    here = lax.axis_index("shard")
    rows = block.shape[0]
    up, down = [block], [block]
    for step in range(1, n):
        up.append(lax.ppermute(up[-1], "shard", [(i, i + 1) for i in range(step - 1, n - 1)]))
        down.append(lax.ppermute(down[-1], "shard", [(i + 1, i) for i in range(n - step)]))
    whole = jnp.zeros((n * rows,) + block.shape[1:], block.dtype)
    whole = lax.dynamic_update_slice_in_dim(whole, block, here * rows, 0)
    for far in range(1, n):
        came = jnp.where(here >= far, up[far], down[n - far])
        whole = lax.dynamic_update_slice_in_dim(whole, came, (here + n - far) % n * rows, 0)
    return whole


def local(grad_parts, first_moment, second_moment, master, old_map, new_map):
    groups = lax.axis_size("dp")
    shard_width = lax.axis_size("shard")
    device_count = groups * shard_width
    my_index = lax.axis_index("dp") * shard_width + lax.axis_index("shard")
    span, block_len = first_moment.shape
    rows = block_len // LANES
    local_blocks = lax.dynamic_slice_in_dim(old_map, my_index * span, span)
    route = owner_table(local_blocks, new_map, device_count, span).T
    wanted = lax.dynamic_slice_in_dim(new_map, my_index * span, span)
    pick = owner_table(wanted, old_map, device_count, span)
    outgoing = [
        jnp.dot(route, a.astype(half), preferred_element_type=full).astype(half).reshape(device_count, rows, LANES)
        for a in (first_moment, second_moment, master)
    ]
    outgoing = jnp.concatenate(outgoing, axis=1)
    incoming = lax.all_to_all(outgoing, ("dp", "shard"), split_axis=0, concat_axis=0, tiled=True)
    summed_grad = sum_over_replicas(grad_parts[0])
    incoming = incoming.reshape(device_count, 3, block_len)
    states = [
        jnp.dot(pick, incoming[:, k], preferred_element_type=full) for k in range(3)
    ]
    new_one, new_two, updated = adamw(*states, summed_grad)
    gathered = gather_line(updated.astype(half))
    return (new_one, new_two, updated, gathered)


def solution(mesh):
    placed = (
        P("dp", None, "shard", None),
        P(("dp", "shard"), None),
        P(("dp", "shard"), None),
        P(("dp", "shard"), None),
        P(),
        P(),
    )
    return jax.shard_map(
        local,
        mesh=mesh,
        in_specs=placed,
        out_specs=(
            P(("dp", "shard"), None),
            P(("dp", "shard"), None),
            P(("dp", "shard"), None),
            P("dp", None),
        ),
        check_vma=False,
    )
```

```python
import jax
import jax.numpy as jnp
from jax import lax
from jax.experimental import pallas as pl
from jax.experimental.pallas import tpu as pltpu
from jax.sharding import PartitionSpec as P


beta_one = 0.9
beta_two = 0.95
learning_rate = 0.05
decay_rate = 0.1
epsilon = 1e-08
step_count = 4
LANES = 128
SUBLANES = 8
CHUNKS = 2
half = jnp.bfloat16
full = jnp.float32
ANY = pl.BlockSpec(memory_space=pl.ANY)
GRANT = pltpu.CompilerParams(vmem_limit_bytes=16 << 20)


def adamw(moment_one, moment_two, weights, gradient):
    new_one = beta_one * moment_one + (1.0 - beta_one) * gradient
    new_two = beta_two * moment_two + (1.0 - beta_two) * gradient * gradient
    unbiased_one = new_one * (1.0 / (1.0 - beta_one**step_count))
    unbiased_two = new_two * (1.0 / (1.0 - beta_two**step_count))
    updated = weights - learning_rate * (
        unbiased_one / (jnp.sqrt(unbiased_two) + epsilon) + decay_rate * weights
    )
    return (new_one, new_two, updated)


def owners(blocks, mapping, span):
    found = blocks[:, :, None] == mapping[:, None, :]
    device = jnp.arange(mapping.shape[1], dtype=jnp.int32) // span
    return jnp.sum(jnp.where(found, device[None, None, :], 0), axis=2)


def in_hbm(array):
    return pltpu.with_memory_space_constraint(array, pltpu.HBM)


def cost(nbytes, flops=0):
    return pl.CostEstimate(flops=flops, bytes_accessed=nbytes, transcendentals=0)


def pack_kernel(dest, *refs):
    arrays, out, rows = refs[:3], refs[-2], refs[-1]
    tiles = arrays[0].shape[1] // LANES
    step = pl.program_id(0)
    for k, array in enumerate(arrays):
        for t in range(tiles):
            rows[k, t * SUBLANES : (t + 1) * SUBLANES] = array[:, t * LANES : (t + 1) * LANES]
    for row in range(SUBLANES):
        to = dest[step * SUBLANES + row]
        for k in range(3):
            line = rows[k, pl.ds(row, tiles, stride=SUBLANES), :]
            out[to, k * tiles : (k + 1) * tiles] = line.astype(half)


def pack(dest, arrays, chunk, width, devices, after):
    span = arrays[0].shape[0]
    tiles = width // LANES
    wide = pl.BlockSpec((SUBLANES, width), lambda i, s: (i, chunk))
    shape = (devices, 3 * tiles, LANES)
    return pl.pallas_call(
        pack_kernel,
        out_shape=jax.ShapeDtypeStruct(shape, half),
        grid_spec=pltpu.PrefetchScalarGridSpec(
            num_scalar_prefetch=1,
            grid=(span // SUBLANES,),
            in_specs=[wide] * 3 + [ANY] * len(after),
            out_specs=pl.BlockSpec(shape, lambda i, s: (0, 0, 0)),
            scratch_shapes=[pltpu.VMEM((3, tiles * SUBLANES, LANES), full)],
        ),
        cost_estimate=cost(18 * span * width),
        compiler_params=GRANT,
    )(dest, *map(in_hbm, arrays), *after)


def send_kernel(bits, grads, *refs):
    refs[-1][...] = grads[...]


def first_send(bits, grads, chunk, width, after):
    groups, span, _ = grads.shape
    return pl.pallas_call(
        send_kernel,
        out_shape=jax.ShapeDtypeStruct((groups // 2, span, width), half),
        grid_spec=pltpu.PrefetchScalarGridSpec(
            num_scalar_prefetch=1,
            grid=(groups // 2,),
            in_specs=[pl.BlockSpec((1, span, width), lambda i, b: (2 * i + 1 - b[0], 0, chunk))] + [ANY] * len(after),
            out_specs=pl.BlockSpec((1, span, width), lambda i, b: (i, 0, 0)),
        ),
        cost_estimate=cost(2 * groups * span * width),
        compiler_params=GRANT,
    )(bits, in_hbm(grads), *after)


def halve_kernel(bits, *refs):
    outs = refs[-4:]
    for k in range(4):
        total = refs[2 * k][...].astype(full) + refs[2 * k + 1][...].astype(full)
        outs[k][...] = total.astype(outs[k].dtype)


def halve(bits, parts, cut, span, after, last):
    specs, operands = [], []
    for kept, kept_at, came, came_col, left, bit in parts:
        place = left[::-1].index(bit)
        for keep in (False, True):

            def combo(i, b, place=place, bit=bit, keep=keep):
                value = b[bit] if keep else 1 - b[bit]
                return ((i >> place) << (place + 1)) | (value << place) | (i & ((1 << place) - 1))

            specs += [
                pl.BlockSpec((1, rows_of(span), cut), lambda i, r, b, combo=combo, at=kept_at: at(combo(i, b), r, b)),
                pl.BlockSpec((1, rows_of(span), cut), lambda i, r, b, combo=combo, col=came_col: (combo(i, b), r, col)),
            ]
            operands += [in_hbm(kept) if kept.ndim == 3 and kept.shape[-1] > cut else kept, came]
    combos = 1 << (len(parts[0][4]) - 1)
    out = pl.BlockSpec((1, rows_of(span), cut), lambda i, r, b: (i, r, 0))
    shape = (combos, span, cut)
    return pl.pallas_call(
        halve_kernel,
        out_shape=[jax.ShapeDtypeStruct(shape, half), jax.ShapeDtypeStruct(shape, full if last else half)] * 2,
        grid_spec=pltpu.PrefetchScalarGridSpec(
            num_scalar_prefetch=1,
            grid=(combos, span // rows_of(span)),
            in_specs=specs + [ANY] * len(after),
            out_specs=[out] * 4,
        ),
        cost_estimate=cost(24 * combos * span * cut),
        compiler_params=GRANT,
    )(bits, *operands, *after)


def rows_of(span):
    return span // 2


def swap(part, bit):
    groups = lax.axis_size("dp")
    return lax.ppermute(part, "dp", [(i, i ^ (1 << bit)) for i in range(groups)])


def update_kernel(source, here, came_in, keep_a, got_a, keep_b, got_b, *refs):
    one_ref, two_ref, master_ref, half_ref, whole_ref, states = refs[-6:]
    tiles = keep_a.shape[2] // LANES
    sub = 2 * tiles
    step = pl.program_id(0)
    for row in range(SUBLANES):
        block = came_in[source[step * SUBLANES + row]].astype(full)
        for k in range(3):
            states[k, pl.ds(row, sub, stride=SUBLANES), :] = block[k * sub : (k + 1) * sub]
    for kept, came, first in ((keep_a, got_a, 0), (keep_b, got_b, tiles)):
        for t in range(tiles):
            cols = slice(t * LANES, (t + 1) * LANES)
            out_cols = slice((first + t) * LANES, (first + t + 1) * LANES)
            rows = slice((first + t) * SUBLANES, (first + t + 1) * SUBLANES)
            gradient = kept[0, :, cols] + came[0, :, cols].astype(full)
            one, two, new = adamw(states[0, rows], states[1, rows], states[2, rows], gradient)
            one_ref[:, out_cols] = one
            two_ref[:, out_cols] = two
            master_ref[:, out_cols] = new
            half_ref[:, out_cols] = new.astype(half)
            whole_ref[:, out_cols] = new.astype(half)


def update(source, here, incoming, terms, carried, chunk, span, block_len, shards, after):
    sub = incoming.shape[1] // 3
    width = sub * LANES
    piece = pl.BlockSpec((1, SUBLANES, width // 2), lambda i, s, h: (0, i, 0))
    wide = pl.BlockSpec((SUBLANES, width), lambda i, s, h: (i, chunk))
    tile_rows = span // SUBLANES
    whole = pl.BlockSpec((SUBLANES, width), lambda i, s, h: (h[0] * tile_rows + i, chunk))
    outs = [jax.ShapeDtypeStruct((span, block_len), full)] * 3 + [
        jax.ShapeDtypeStruct((span, width), half),
        jax.ShapeDtypeStruct((shards * span, block_len), half),
    ]
    spread = {7 + i: o for i, o in enumerate((0, 1, 2, 4))} if carried else {}
    return pl.pallas_call(
        update_kernel,
        out_shape=outs,
        grid_spec=pltpu.PrefetchScalarGridSpec(
            num_scalar_prefetch=2,
            grid=(tile_rows,),
            in_specs=[pl.BlockSpec(incoming.shape, lambda i, s, h: (0, 0, 0))]
            + [piece] * 4
            + [ANY] * (len(carried) + len(after)),
            out_specs=[wide] * 3 + [pl.BlockSpec((SUBLANES, width), lambda i, s, h: (i, 0)), whole],
            scratch_shapes=[pltpu.VMEM((3, sub * SUBLANES, LANES), full)],
        ),
        input_output_aliases=spread,
        cost_estimate=cost(26 * span * width, 20 * span * width),
        compiler_params=GRANT,
    )(source, here, in_hbm(incoming), *map(in_hbm, terms), *carried, *after)


def exchange(outgoing):
    return lax.all_to_all(outgoing, ("dp", "shard"), split_axis=0, concat_axis=0, tiled=True)


def gather_steps(block, last):
    n = lax.axis_size("shard")
    up, down = {0: block}, {0: block}
    if last and n == 4:
        near = lax.ppermute(block, "shard", [(i, (i + 1) % n) for i in range(n)])
        back = lax.ppermute(block, "shard", [((i + 1) % n, i) for i in range(n)])
        over = lax.ppermute(near, "shard", [(i, i + 1) for i in range(1, n - 1)])
        under = lax.ppermute(back, "shard", [(i + 1, i) for i in range(n - 2)])
        return {1: (near, near), 3: (back, back), 2: (over, under)}
    for step in range(1, n):
        up[step] = lax.ppermute(up[step - 1], "shard", [(i, i + 1) for i in range(step - 1, n - 1)])
        down[step] = lax.ppermute(down[step - 1], "shard", [(i + 1, i) for i in range(n - step)])
    return {far: (up[far], down[n - far]) for far in range(1, n)}


def place(whole, came, column):
    n = lax.axis_size("shard")
    here = lax.axis_index("shard")
    for far, (below, above) in came.items():
        value = below if below is above else jnp.where(here >= far, below, above)
        whole = lax.dynamic_update_slice(whole, value, ((here + n - far) % n * value.shape[0], column))
    return whole


def local(grad_parts, first_moment, second_moment, master, old_map, new_map):
    groups = lax.axis_size("dp")
    shards = lax.axis_size("shard")
    devices = groups * shards
    here = lax.axis_index("shard")
    replica = lax.axis_index("dp")
    mine = replica * shards + here
    span, block_len = first_moment.shape
    chunks = CHUNKS if block_len % (CHUNKS * 2 * SUBLANES * LANES) == 0 else 1
    width = block_len // chunks
    cut = width // 2
    grads = grad_parts[0]
    maps = jnp.stack([old_map, new_map])
    dest, source = owners(lax.dynamic_slice_in_dim(maps, mine * span, span, 1), maps[::-1], span)
    at = here.reshape(1).astype(jnp.int32)
    steps = groups.bit_length() - 1
    bits = ((replica >> jnp.arange(steps, dtype=jnp.int32)) & 1).astype(jnp.int32)
    left = list(range(steps))[::-1][:-1]
    orders = (left[::-1], left)
    states = (first_moment, second_moment, master)

    def first_parts(c, came):
        return [
            (grads, lambda j, r, b, h=h: (2 * j + b[0], r, 2 * c + h), came, h, left, orders[h][0]) for h in range(2)
        ]

    def next_parts(c, s, came):
        return [
            (sums[c][2 * h + 1], lambda j, r, b: (j, r, 0), came[h], 0, [b for b in left if b not in orders[h][:s]], orders[h][s])
            for h in range(2)
        ]

    def swaps(c, s):
        return [swap(sums[c][2 * h], orders[h][s]) for h in range(2)]

    def finish_sum(c, after):
        for s in range(1, len(left)):
            came = swaps(c, s - 1)
            sums[c] = halve(bits, next_parts(c, s, came), cut, span, after, s == len(left) - 1)
            after = [sums[c][0]]
        return after

    outgoing, incoming, pair, sums, carried = {}, {}, {}, {}, []
    last = chunks - 1
    short = len(left) == 1
    outgoing[0] = pack(dest, states, 0, width, devices, [])
    incoming[0] = exchange(outgoing[0])
    after = [outgoing[0]]
    for c in range(chunks):
        sent = first_send(bits, grads, c, width, after)
        after = [sent]
        pair[c] = swap(sent, 0)
    sums[0] = halve(bits, first_parts(0, pair[0]), cut, span, after, short)
    after = [sums[0][0]]
    for c in range(1, chunks):
        outgoing[c] = pack(dest, states, c, width, devices, after)
        after = [outgoing[c]]
        sums[c] = halve(bits, first_parts(c, pair[c]), cut, span, after, short)
        after = [sums[c][0]]
    after = finish_sum(0, after)
    gathered = []
    for c in range(chunks):
        if c < last:
            incoming[c + 1] = exchange(outgoing[c + 1])
        came = swaps(c, len(left) - 1)
        terms = [sums[c][1], came[0], sums[c][3], came[1]]
        one, two, new, block, whole = update(source, at, incoming[c], terms, carried, c, span, block_len, shards, after)
        carried = [one, two, new, whole]
        after = [block]
        gathered.append(gather_steps(block, c == last))
        if c < last:
            after = finish_sum(c + 1, after) + [gathered[c][1][0]]
    for c in range(chunks):
        whole = place(whole, gathered[c], c * width)
    return (one, two, new, whole)


def solution(mesh):
    placed = (
        P("dp", None, "shard", None),
        P(("dp", "shard"), None),
        P(("dp", "shard"), None),
        P(("dp", "shard"), None),
        P(),
        P(),
    )
    return jax.shard_map(
        local,
        mesh=mesh,
        in_specs=placed,
        out_specs=(
            P(("dp", "shard"), None),
            P(("dp", "shard"), None),
            P(("dp", "shard"), None),
            P("dp", None),
        ),
        check_vma=False,
    )
```

```python
import functools
import jax
import jax.numpy as jnp
from jax import lax
from jax.experimental import pallas as pl
from jax.experimental.pallas import tpu as pltpu
from jax.sharding import PartitionSpec as P


beta_one = 0.9
beta_two = 0.95
learning_rate = 0.05
decay_rate = 0.1
epsilon = 1e-08
step_count = 4
LANES = 128
SUBLANES = 8
PARTS = (3, 1)
half = jnp.bfloat16
full = jnp.float32
ANY = pl.BlockSpec(memory_space=pl.ANY)
GRANT = pltpu.CompilerParams(vmem_limit_bytes=16 << 20)


def adamw(moment_one, moment_two, weights, gradient):
    new_one = beta_one * moment_one + (1.0 - beta_one) * gradient
    new_two = beta_two * moment_two + (1.0 - beta_two) * gradient * gradient
    unbiased_one = new_one * (1.0 / (1.0 - beta_one**step_count))
    unbiased_two = new_two * (1.0 / (1.0 - beta_two**step_count))
    updated = weights - learning_rate * (
        unbiased_one / (jnp.sqrt(unbiased_two) + epsilon) + decay_rate * weights
    )
    return (new_one, new_two, updated)


def owners(blocks, mapping, span):
    device = jnp.arange(mapping.shape[1], dtype=jnp.int32) // span
    found = blocks[:, :, None] == mapping[:, None, :]
    return jnp.sum(jnp.where(found, device[None, None, :], 0), axis=2)


def in_hbm(array):
    return pltpu.with_memory_space_constraint(array, pltpu.HBM)


def block(shape, where, start):
    width = shape[-1]
    if start % width == 0:
        return pl.BlockSpec(shape, lambda *at: (*where(*at), start // width))
    return pl.BlockSpec(
        tuple(pl.Element(size) for size in shape),
        lambda *at: (*(index * size for index, size in zip(where(*at), shape)), start),
    )


def cost(nbytes, flops=0):
    return pl.CostEstimate(flops=flops, bytes_accessed=nbytes, transcendentals=0)


def pack_kernel(by_shard, shards, dest, here, *refs):
    arrays, row_of = refs[:3], refs[-1]
    bands, depth, _ = arrays[0].shape
    span, sub = bands * SUBLANES, depth // SUBLANES
    outs = refs[3:-1]
    per_out = span // len(outs)

    @pl.when(pl.program_id(0) == 0)
    def _():
        for row in range(span):
            to = dest[row]
            if by_shard:
                to = lax.rem(lax.rem(to, shards) - here[0] + shards, shards) * per_out + lax.div(to, shards)
            row_of[to] = row

    for o, out in enumerate(outs):
        for slot in range(per_out):
            row = row_of[o * per_out + slot]
            band, first = lax.div(row, SUBLANES), lax.rem(row, SUBLANES)
            for k, array in enumerate(arrays):
                out[slot, k] = array[band, pl.ds(first, sub, stride=SUBLANES), :].astype(half)


def by_tile(array):
    span, width = array.shape
    tiled = array.reshape(span // SUBLANES, SUBLANES, width // LANES, LANES).transpose(0, 2, 1, 3)
    return tiled.reshape(span // SUBLANES, width // LANES * SUBLANES, LANES)


def pack(dest, here, arrays, start, width, shards, by_shard):
    span = arrays[0].shape[0]
    bands, tiles = span // SUBLANES, width // LANES
    steps = max(1, min(tiles // 16, 2))
    sub = tiles // steps
    count = shards if by_shard else 1
    deep = pl.BlockSpec((bands, sub * SUBLANES, LANES), lambda i, s, h: (0, start // (sub * LANES) + i, 0))
    shape = (span // count, 3, tiles, LANES)
    return pl.pallas_call(
        functools.partial(pack_kernel, by_shard, shards),
        out_shape=[jax.ShapeDtypeStruct(shape, half)] * count,
        grid_spec=pltpu.PrefetchScalarGridSpec(
            num_scalar_prefetch=2,
            grid=(steps,),
            in_specs=[deep] * 3,
            out_specs=[pl.BlockSpec((span // count, 3, sub, LANES), lambda i, s, h: (0, 0, i, 0))] * count,
            scratch_shapes=[pltpu.SMEM((span,), jnp.int32)],
        ),
        cost_estimate=cost(18 * span * width),
        compiler_params=GRANT,
    )(dest, here, *(in_hbm(by_tile(array)) for array in arrays))


def send_kernel(bits, grads, *refs):
    refs[-1][...] = grads[...]


def first_send(bits, grads, start, width):
    groups, span, _ = grads.shape
    return pl.pallas_call(
        send_kernel,
        out_shape=jax.ShapeDtypeStruct((groups // 2, span, width), half),
        grid_spec=pltpu.PrefetchScalarGridSpec(
            num_scalar_prefetch=1,
            grid=(groups // 2,),
            in_specs=[block((1, span, width), lambda i, b: (2 * i + 1 - b[0], 0), start)],
            out_specs=pl.BlockSpec((1, span, width), lambda i, b: (i, 0, 0)),
        ),
        cost_estimate=cost(2 * groups * span * width),
        compiler_params=GRANT,
    )(bits, in_hbm(grads))


def halve_kernel(bits, *refs):
    outs = refs[-4:]
    for k in range(4):
        total = refs[2 * k][...].astype(full) + refs[2 * k + 1][...].astype(full)
        outs[k][...] = total.astype(outs[k].dtype)


def halve(bits, parts, cut, span, last):
    specs, operands = [], []
    for kept, group, kept_col, came, came_col, left, bit in parts:
        place = left[::-1].index(bit)
        for keep in (False, True):

            def combo(i, b, place=place, bit=bit, keep=keep):
                value = b[bit] if keep else 1 - b[bit]
                return ((i >> place) << (place + 1)) | (value << place) | (i & ((1 << place) - 1))

            specs += [
                block((1, rows_of(span), cut), lambda i, r, b, combo=combo, group=group: (group(combo(i, b), b), r), kept_col),
                pl.BlockSpec((1, rows_of(span), cut), lambda i, r, b, combo=combo, col=came_col: (combo(i, b), r, col)),
            ]
            operands += [in_hbm(kept) if kept.ndim == 3 and kept.shape[-1] > cut else kept, came]
    combos = 1 << (len(parts[0][5]) - 1)
    out = pl.BlockSpec((1, rows_of(span), cut), lambda i, r, b: (i, r, 0))
    shape = (combos, span, cut)
    return pl.pallas_call(
        halve_kernel,
        out_shape=[jax.ShapeDtypeStruct(shape, half), jax.ShapeDtypeStruct(shape, full if last else half)] * 2,
        grid_spec=pltpu.PrefetchScalarGridSpec(
            num_scalar_prefetch=1,
            grid=(combos, span // rows_of(span)),
            in_specs=specs,
            out_specs=[out] * 4,
        ),
        cost_estimate=cost(24 * combos * span * cut),
        compiler_params=GRANT,
    )(bits, *operands)


def rows_of(span):
    return span // 2


def swap(part, bit):
    groups = lax.axis_size("dp")
    return lax.ppermute(part, "dp", [(i, i ^ (1 << bit)) for i in range(groups)])


def update_kernel(whole_step, source, here, *refs):
    rows_in, (keep_a, got_a, keep_b, got_b), states = refs[:SUBLANES], refs[SUBLANES : SUBLANES + 4], refs[-1]
    tiles = keep_a.shape[2] // LANES
    sub = 2 * tiles
    for row, row_in in enumerate(rows_in):
        came = row_in[0].astype(full)
        for k in range(3):
            states[k, pl.ds(row, sub, stride=SUBLANES), :] = came[k * sub : (k + 1) * sub]
    for kept, came, first in ((keep_a, got_a, 0), (keep_b, got_b, tiles)):
        for t in range(tiles):
            cols = slice(t * LANES, (t + 1) * LANES)
            out_cols = slice((first + t) * LANES, (first + t + 1) * LANES)
            rows = slice((first + t) * SUBLANES, (first + t + 1) * SUBLANES)
            gradient = kept[0, :, cols] + came[0, :, cols].astype(full)
            values = adamw(states[0, rows], states[1, rows], states[2, rows], gradient)
            if whole_step:
                for ref, value in zip(refs[-5:-1], values + values[2:]):
                    ref[:, out_cols] = value.astype(ref.dtype)
            else:
                refs[-2][:, out_cols] = values[2].astype(half)


def update(source, here, incoming, terms, carried, chunk, start, span, block_len, shards, by_shard, whole_step):
    sub = incoming.shape[1] // 3
    width = sub * LANES
    piece = pl.BlockSpec((1, SUBLANES, width // 2), lambda i, s, h: (0, i, 0))
    tile_rows = span // SUBLANES
    spread = {}

    def row_at(row):
        def index(i, s, h):
            at = s[i * SUBLANES + row]
            if by_shard:
                at = lax.div(at, shards) * shards + lax.rem(h[0] - lax.rem(at, shards) + shards, shards)
            return (at, 0, 0)

        return index

    if whole_step:
        wide = block((SUBLANES, width), lambda i, s, h: (i,), start)
        out_specs = [wide] * 3 + [block((SUBLANES, width), lambda i, s, h: (h[0] * tile_rows + i,), start)]
        outs = [jax.ShapeDtypeStruct((span, block_len), full)] * 3
        outs += [jax.ShapeDtypeStruct((shards * span, block_len), half)]
        if carried:
            spread = {6 + SUBLANES + o: o for o in range(4)}
    else:
        out_specs = [pl.BlockSpec((SUBLANES, width), lambda i, s, h: (i, 0))]
        outs = [jax.ShapeDtypeStruct((span, width), half)]
    call = pl.pallas_call(
        functools.partial(update_kernel, whole_step),
        out_shape=outs,
        grid_spec=pltpu.PrefetchScalarGridSpec(
            num_scalar_prefetch=2,
            grid=(tile_rows,),
            in_specs=[pl.BlockSpec((1, 3 * sub, LANES), row_at(row)) for row in range(SUBLANES)]
            + [piece] * 4
            + [ANY] * len(carried),
            out_specs=out_specs,
            scratch_shapes=[pltpu.VMEM((3, sub * SUBLANES, LANES), full)],
        ),
        input_output_aliases=spread,
        cost_estimate=cost(26 * span * width, 20 * span * width),
        compiler_params=GRANT,
    )
    held = in_hbm if chunk == 0 else lambda array: array
    return call(source, here, *[held(incoming)] * SUBLANES, *map(held, terms), *carried)


def exchange(outgoing):
    devices, _, tiles, _ = outgoing.shape
    came = lax.all_to_all(outgoing.reshape(devices, 3 * tiles, LANES), ("dp", "shard"), split_axis=0, concat_axis=0, tiled=True)
    return came


def travel(outgoing):
    n = lax.axis_size("shard")
    came = [outgoing[0]]
    for far in range(1, n):
        came.append(lax.ppermute(outgoing[far], "shard", [(i, (i + far) % n) for i in range(n)]))
    return came


def spread(came):
    groups, _, tiles, _ = came[0].shape
    stacked = jnp.stack(came, axis=1).reshape(groups, len(came) * 3 * tiles, LANES)
    came = lax.all_to_all(stacked, "dp", split_axis=0, concat_axis=0, tiled=True)
    return came.reshape(-1, 3 * tiles, LANES)


def gather_steps(block, direct):
    n = lax.axis_size("shard")

    def rotate(far):
        return lax.ppermute(block, "shard", [(i, (i + far) % n) for i in range(n)])

    if direct:
        return {far: (rotate(far),) * 2 for far in range(1, n)}
    if n == 4:
        near, back = rotate(1), rotate(3)
        over = lax.ppermute(near, "shard", [(i, i + 1) for i in range(1, n - 1)])
        under = lax.ppermute(back, "shard", [(i + 1, i) for i in range(n - 2)])
        return {1: (near, near), 3: (back, back), 2: (over, under)}
    up, down = {0: block}, {0: block}
    for step in range(1, n):
        up[step] = lax.ppermute(up[step - 1], "shard", [(i, i + 1) for i in range(step - 1, n - 1)])
        down[step] = lax.ppermute(down[step - 1], "shard", [(i + 1, i) for i in range(n - step)])
    return {far: (up[far], down[n - far]) for far in range(1, n)}


def place(whole, came, column):
    n = lax.axis_size("shard")
    here = lax.axis_index("shard")
    for far, (below, above) in came.items():
        value = below if below is above else jnp.where(here >= far, below, above)
        whole = lax.dynamic_update_slice(whole, value, ((here + n - far) % n * value.shape[0], column))
    return whole


def local(grad_parts, first_moment, second_moment, master, old_map, new_map):
    groups = lax.axis_size("dp")
    shards = lax.axis_size("shard")
    here = lax.axis_index("shard")
    replica = lax.axis_index("dp")
    mine = replica * shards + here
    span, block_len = first_moment.shape
    unit = block_len // sum(PARTS)
    parts_of = PARTS if unit % (2 * SUBLANES * LANES) == 0 else (1,)
    widths = [p * (block_len // sum(parts_of)) for p in parts_of]
    starts = [sum(widths[:c]) for c in range(len(widths))]
    chunks = len(widths)
    grads = grad_parts[0]
    maps = jnp.stack([old_map, new_map])
    dest, source = owners(lax.dynamic_slice_in_dim(maps, mine * span, span, 1), maps[::-1], span)
    at = here.reshape(1).astype(jnp.int32)
    steps = groups.bit_length() - 1
    bits = ((replica >> jnp.arange(steps, dtype=jnp.int32)) & 1).astype(jnp.int32)
    left = list(range(steps))[::-1][:-1]
    orders = (left[::-1], left)
    states = (first_moment, second_moment, master)

    def first_parts(c, came):
        return [
            (grads, lambda j, b: 2 * j + b[0], starts[c] + h * (widths[c] // 2), came, h, left, orders[h][0])
            for h in range(2)
        ]

    def next_parts(c, s, came):
        return [
            (sums[c][2 * h + 1], lambda j, b: j, 0, came[h], 0, [b for b in left if b not in orders[h][:s]], orders[h][s])
            for h in range(2)
        ]

    def swaps(c, s):
        return [swap(sums[c][2 * h], orders[h][s]) for h in range(2)]

    def summed(c):
        cut = widths[c] // 2
        came = swap(first_send(bits, grads, starts[c], widths[c]), 0)
        sums[c] = halve(bits, first_parts(c, came), cut, span, len(left) == 1)
        for s in range(1, len(left)):
            sums[c] = halve(bits, next_parts(c, s, swaps(c, s - 1)), cut, span, s == len(left) - 1)
        came = swaps(c, len(left) - 1)
        return [sums[c][1], came[0], sums[c][3], came[1]]

    sums, carried, gathered = {}, [], []
    for c in range(chunks):
        split = c > 0
        outgoing = pack(dest, at, states, starts[c], widths[c], shards, split)
        if split:
            incoming = spread(travel(outgoing))
        else:
            incoming = exchange(outgoing[0])
        given = (source, at, incoming, summed(c))
        sizes = (c, starts[c], span, block_len, shards, split)
        (weights,) = update(*given, [], *sizes, False)
        gathered.append(gather_steps(weights, False))
        carried = update(*given, carried, *sizes, True)
    one, two, new, whole = carried
    for c in range(chunks):
        whole = place(whole, gathered[c], starts[c])
    return (one, two, new, whole)


def solution(mesh):
    placed = (
        P("dp", None, "shard", None),
        P(("dp", "shard"), None),
        P(("dp", "shard"), None),
        P(("dp", "shard"), None),
        P(),
        P(),
    )
    return jax.shard_map(
        local,
        mesh=mesh,
        in_specs=placed,
        out_specs=(
            P(("dp", "shard"), None),
            P(("dp", "shard"), None),
            P(("dp", "shard"), None),
            P("dp", None),
        ),
        check_vma=False,
    )
```
